512 devices in a mesh: clip: 4 (over y), frame: 8 (over x, z_hi), pix: 16 (over z_lo, core).
Axes of the slice: x: 4, y: 4, z: 16 (z_hi: 2, z_lo: 8; z = z_hi * 8 + z_lo), core: 2. Of those that a mesh axis runs over, the one named last changes fastest.
Arguments:
- features: bfloat16 [32, 32, 96, 256], P(('clip', 'frame'), 'pix'), parts along dimension 0, may hold values from -6 to 6
Outputs:
- forward_full: bfloat16 [32, 32, 96, 3072], P(('clip', 'frame'), 'pix'), parts along dimension 0
- forward_half: bfloat16 [32, 32, 96, 768], P(('clip', 'frame'), 'pix'), parts along dimension 0
- forward_quarter: bfloat16 [32, 32, 96, 192], P(('clip', 'frame'), 'pix'), parts along dimension 0
- forward_eighth: bfloat16 [32, 32, 96, 48], P(('clip', 'frame'), 'pix'), parts along dimension 0
- backward_full: bfloat16 [32, 32, 96, 3072], P(('clip', 'frame'), 'pix'), parts along dimension 0
- backward_half: bfloat16 [32, 32, 96, 768], P(('clip', 'frame'), 'pix'), parts along dimension 0
- backward_quarter: bfloat16 [32, 32, 96, 192], P(('clip', 'frame'), 'pix'), parts along dimension 0
- backward_eighth: bfloat16 [32, 32, 96, 48], P(('clip', 'frame'), 'pix'), parts along dimension 0
The draws below stay inside these ranges and needn't reach their ends.
There are 4 independent parts, one for each index of `clip`. The reference program is written for one: setup_inputs(seed, part) draws one part's arguments, and reference() takes and returns one part's arrays. A program takes and returns all parts, laid end to end along the dimension named above; each array names one. Nothing has to cross between parts.
All inputs are finite; a program needn't handle non-finite values.
Results may differ from the reference program's by a relative error of at most 0.001.
Values may be sent and summed in bfloat16 or wider, within the bound.
A program may use at most 64 MiB of HBM per device.

```python
import math
import jax
import jax.numpy as jnp
from jax import lax

C = 256
W = 96
H = 32
FRAMES = 8


def levels(stream_key, shape, shards, low, high):
    level, own = 1.0, jax.random.fold_in(stream_key, 6)
    for dim, parts in shards:
        draws = jnp.exp(jax.random.uniform(jax.random.fold_in(own, dim), (parts,), jnp.float32, low / len(shards), high / len(shards)))
        level = level * jnp.repeat(draws, shape[dim] // parts).reshape([-1 if axis == dim else 1 for axis in range(len(shape))])
    return level


def centred(rng, shape, deviation, most, cuts=(), kind=jnp.bfloat16):
    factor_of = levels(rng, shape, cuts, -0.22, 0.18) if cuts else 1.0
    array = jax.random.normal(rng, shape, jnp.float32) * deviation * factor_of
    return jnp.minimum(jnp.maximum(array, -most), most).astype(kind)


def setup_inputs(seed: int = 0, part: int = 0) -> dict:
    arg_keys = jax.random.split(jax.random.key(seed), 2)
    part_keys = jax.random.split(jax.random.fold_in(arg_keys[1], part), 2)
    return {
        "features": centred(part_keys[0], (FRAMES, H, W, C), 1.0, 6.0, ((0, 8), (1, 16))),
    }


def halved(current):
    count, height, breadth = current.shape
    return current.reshape(count, height // 2, 2, breadth // 2, 2).mean(axis=(2, 4))

def pyramid_of(frame_now, target):
    own_pixels = frame_now.reshape(H * W, C)
    target_pixels = target.reshape(H * W, C)
    scores = jnp.dot(own_pixels, target_pixels.T, preferred_element_type=jnp.float32) * (1.0 / math.sqrt(C))
    current = scores.reshape(H * W, H, W)
    result = []
    for depth_index in range(4):
        result.append(current.reshape(H, W, -1).astype(jnp.bfloat16))
        if depth_index < 3:
            current = halved(current)
    return tuple(result)

def pair_pyramid(paired):
    return pyramid_of(paired[0], paired[1])

def reference(features):
    blank = jnp.zeros((1, H, W, C), features.dtype)
    following = jnp.concatenate([features[1:], blank], axis=0)
    preceding = jnp.concatenate([blank, features[:-1]], axis=0)
    forward = lax.map(pair_pyramid, (features, following))
    backward = lax.map(pair_pyramid, (features, preceding))
    return (forward[0], forward[1], forward[2], forward[3], backward[0], backward[1], backward[2], backward[3])
```

```python
import functools
import math

import jax
import jax.numpy as jnp
from jax import lax
from jax.experimental import pallas as pl
from jax.experimental.pallas import tpu as pltpu
from jax.sharding import PartitionSpec as P

MESH = pl.DeviceIdType.MESH
HOP = 2
SIDE = 2


def gather_kernel(frames, line, own, t, init_send, chain_send, x_send, p_send, chain_recv, x_recv, p_recv):
    half = own.shape[0] // 2
    reach = line // 2
    chunks = 2 * reach
    f = lax.axis_index("frame")
    p = lax.axis_index("pix")
    l = p // 2
    c = p % 2
    odd = f % 2
    sign = 1 - 2 * odd
    mate = f + sign
    other = (f - sign + frames) % frames
    ahead = (f + 2 * sign + frames) % frames
    behind = (f - 2 * sign + frames) % frames

    def at(frame, chip, core):
        return {"frame": frame, "pix": 2 * chip + core}

    barrier = pltpu.get_barrier_semaphore()

    def greet(frame, chip, core):
        pl.semaphore_signal(barrier, inc=1, device_id=at(frame, chip, core), device_id_type=MESH)

    greet(f, l, 1 - c)
    greet(ahead, l, c)
    greet(behind, l, c)

    @pl.when(l < line - 1)
    def _():
        greet(f, l + 1, c)

    @pl.when(l > 0)
    def _():
        greet(f, l - 1, c)

    @pl.when(l == line - 1)
    def _():
        for r in range(reach):
            greet(mate, r, c)
            greet(other, r, c)

    @pl.when(l == 0)
    def _():
        for r in range(reach):
            greet(mate, line - 1 - r, c)
            greet(other, line - 1 - r, c)

    inner = jnp.where((l > 0) & (l < line - 1), 1, 0)
    pl.semaphore_wait(barrier, 6 + inner)

    def place(slot, d, r, kind, core):
        source = jnp.where(d == 0, r, line - 1 - r)
        return t.at[slot, 2 * source + core, pl.ds(pl.multiple_of(kind * half, half), half)]

    my_d = jnp.where(l < reach, 0, 1)
    my_r = jnp.where(l < reach, l, line - 1 - l)
    entry = jnp.where(l < reach, line - 1, 0)

    def first(kind):
        return pltpu.make_async_remote_copy(
            src_ref=own.at[pl.ds(kind * half, half)],
            dst_ref=place(odd if kind else 1 - odd, my_d, my_r, kind, c),
            send_sem=init_send.at[kind],
            recv_sem=chain_recv.at[my_d, 2 * my_r + kind],
            device_id=at(other if kind else mate, entry, c),
            device_id_type=MESH,
        )

    def slot_of(kind):
        return jnp.where(kind == 0, odd, 1 - odd)

    def chained(d, k):
        r, kind = k // 2, k % 2
        ref = place(slot_of(kind), d, r, kind, c)
        return pltpu.make_async_remote_copy(
            src_ref=ref,
            dst_ref=ref,
            send_sem=chain_send.at[d, k],
            recv_sem=chain_recv.at[d, k],
            device_id=at(f, jnp.where(d == 0, jnp.maximum(l - 1, 0), jnp.minimum(l + 1, line - 1)), c),
            device_id_type=MESH,
        )

    def sideways(d, k):
        r, kind = k // 2, k % 2
        return pltpu.make_async_remote_copy(
            src_ref=place(slot_of(kind), d, r, kind, c),
            dst_ref=place(1 - slot_of(kind), d, r, kind, c),
            send_sem=x_send.at[d, k],
            recv_sem=x_recv.at[d, k],
            device_id=at(jnp.where(kind == 0, ahead, behind), l, c),
            device_id_type=MESH,
        )

    def across(via, d, k):
        r, kind = k // 2, k % 2
        slot = slot_of(kind)
        ref = place(jnp.where(via == 0, slot, 1 - slot), d, r, kind, c)
        return pltpu.make_async_remote_copy(
            src_ref=ref,
            dst_ref=ref,
            send_sem=p_send.at[via, d, k],
            recv_sem=p_recv.at[via, d, k],
            device_id=at(f, l, 1 - c),
            device_id_type=MESH,
        )

    first(0).start()
    first(1).start()

    def steps_from_entry(d):
        return line - 1 - l if d == 0 else l

    @pl.loop(0, chunks + HOP * (line - 1) + SIDE)
    def _(n):
        for d in (0, 1):
            k = n - HOP * steps_from_entry(d)

            @pl.when((k >= 0) & (k < chunks))
            def _():
                chained(d, k).wait_recv()

                @pl.when(steps_from_entry(d) < line - 1)
                def _():
                    chained(d, k).start()

                sideways(d, k).start()
                across(0, d, k).start()

        for d in (0, 1):
            kx = n - HOP * steps_from_entry(d) - SIDE

            @pl.when((kx >= 0) & (kx < chunks))
            def _():
                sideways(d, kx).wait_recv()
                across(1, d, kx).start()

    @pl.loop(0, chunks)
    def _(k):
        for d in (0, 1):
            for via in (0, 1):
                across(via, d, k).wait_recv()

    first(0).wait_send()
    first(1).wait_send()

    @pl.loop(0, chunks)
    def _(k):
        for d in (0, 1):
            @pl.when(steps_from_entry(d) < line - 1)
            def _():
                chained(d, k).wait_send()

            sideways(d, k).wait_send()
            for via in (0, 1):
                across(via, d, k).wait_send()


def gather(own, frames, line):
    chunks = line
    dma = pltpu.SemaphoreType.DMA
    return pl.pallas_call(
        functools.partial(gather_kernel, frames, line),
        out_shape=jax.ShapeDtypeStruct((2, 2 * line, *own.shape), own.dtype),
        in_specs=[pl.BlockSpec(memory_space=pltpu.VMEM)],
        out_specs=pl.BlockSpec(memory_space=pltpu.VMEM),
        scratch_shapes=[
            dma((2,)),
            dma((2, chunks)),
            dma((2, chunks)),
            dma((2, 2, chunks)),
            dma((2, chunks)),
            dma((2, chunks)),
            dma((2, 2, chunks)),
        ],
        compiler_params=pltpu.CompilerParams(collective_id=0, has_side_effects=True),
        name="gather",
    )(own)


def pooling(out_rows, out_breadth):
    shape = (out_rows * out_breadth, 4 * out_rows * out_breadth)
    i = lax.broadcasted_iota(jnp.int32, shape, 0)
    q = lax.broadcasted_iota(jnp.int32, shape, 1)
    breadth = 2 * out_breadth
    row, column = q // breadth, q % breadth
    same = (row // 2 == i // out_breadth) & (column // 2 == i % out_breadth)
    return jnp.where(same, 0.25, 0.0).astype(jnp.bfloat16)


NT = (((1,), (1,)), ((), ()))


def dot(a, b):
    return jnp.dot(a, b, preferred_element_type=jnp.float32)


def dot_nt(a, b):
    return lax.dot_general(a, b, NT, preferred_element_type=jnp.float32)


def pyramid_kernel(frames, breadth, own, t, *rest):
    outs, (high1, low1, high2, low2) = rest[:8], rest[8:]
    f = lax.axis_index("frame")
    pixels = own.shape[0]
    rows = pixels // breadth
    targets = t.shape[1]
    factor = 1.0 / math.sqrt(own.shape[1])

    def put(ref, start, values):
        size = values.shape[1]
        for row in range(rows):
            ref[0, row, :, start:start + size] = values[row * breadth:(row + 1) * breadth]

    pool1 = pooling(1, breadth // 2)
    pool2 = pooling(2, breadth // 4)
    pool3 = pooling(4, breadth // 8)
    small = pool1.shape[0]

    def split(values):
        high = values.astype(jnp.bfloat16)
        return high, (values - high.astype(jnp.float32)).astype(jnp.bfloat16)

    for slot in (0, 1):
        valid = jnp.where(f < frames - 1, 1, 0) if slot == 0 else jnp.where(f > 0, 1, 0)
        scale = valid.astype(jnp.float32) * factor
        full, half, quarter, eighth = outs[4 * slot:4 * slot + 4]
        tile = 4 * pixels
        for start in range(0, targets, tile):
            scores = dot_nt(own[...], t[slot, start:start + tile])
            put(full, start, (scores * scale).astype(jnp.bfloat16))
        for u in range(targets // pixels):
            values = dot(pool1, t[slot, u * pixels:(u + 1) * pixels])
            high1[slot, u * small:(u + 1) * small], low1[slot, u * small:(u + 1) * small] = split(values)
        for u in range(targets // 4 // pixels):
            at = slice(u * pixels, (u + 1) * pixels)
            values = dot(pool2, high1[slot, at]) + dot(pool2, low1[slot, at])
            high2[slot, u * small:(u + 1) * small], low2[slot, u * small:(u + 1) * small] = split(values)
        high3, low3 = split(dot(pool3, high2[slot]) + dot(pool3, low2[slot]))
        for ref, high, low in ((half, high1[slot], low1[slot]), (quarter, high2[slot], low2[slot])):
            scores = dot_nt(own[...], high) + dot_nt(own[...], low)
            put(ref, 0, (scores * scale).astype(jnp.bfloat16))
        for row in range(rows):
            mine = own[row * breadth:(row + 1) * breadth]
            scores = dot_nt(high3, mine) + dot_nt(low3, mine)
            eighth[0, row] = (scores * scale).astype(jnp.bfloat16)


def pyramids(own, t, frames, rows, breadth):
    targets = t.shape[1]
    depths = [jax.ShapeDtypeStruct((1, rows, breadth, targets // 4**k), jnp.bfloat16) for k in range(3)]
    depths.append(jax.ShapeDtypeStruct((1, rows, targets // 64, breadth), jnp.bfloat16))
    scratch = [pltpu.VMEM((2, targets // 4**k, own.shape[1]), jnp.bfloat16) for k in (1, 1, 2, 2)]
    return pl.pallas_call(
        functools.partial(pyramid_kernel, frames, breadth),
        out_shape=depths * 2,
        in_specs=[pl.BlockSpec(memory_space=pltpu.VMEM)] * 2,
        out_specs=[pl.BlockSpec(memory_space=pltpu.VMEM)] * 8,
        scratch_shapes=scratch,
        name="pyramids",
    )(own, t)


def solution(mesh):
    frames = mesh.shape["frame"]
    line = mesh.shape["pix"] // 2

    def per_device(features):
        _, rows, breadth, channels = features.shape
        own = features.reshape(rows * breadth, channels)
        t = gather(own, frames, line)
        t = t.reshape(2, -1, channels)
        outs = list(pyramids(own, t, frames, rows, breadth))
        for k in (3, 7):
            outs[k] = outs[k].swapaxes(2, 3)
        return tuple(outs)

    spec = P(("clip", "frame"), "pix", None, None)
    return jax.shard_map(per_device, mesh=mesh, in_specs=(spec,), out_specs=(spec,) * 8, check_vma=False)
```

```python
import functools
import math

import jax
import jax.numpy as jnp
from jax import lax
from jax.experimental import pallas as pl
from jax.experimental.pallas import tpu as pltpu
from jax.sharding import PartitionSpec as P

MESH = pl.DeviceIdType.MESH
SUB = 1
SIDE = 8
SWAP = 1
EARLY = 1
UNROLL = True
MID = 2


def gather_kernel(frames, line, own, t, init_send, on_send, back_send, x_send, p_send, chain_recv, x_recv, p_recv):
    half = own.shape[0] // 2
    piece = half // SUB
    reach = line // 2
    chunks = 4 * SUB * reach
    f = lax.axis_index("frame")
    p = lax.axis_index("pix")
    l = p // 2
    c = p % 2
    odd = f % 2
    sign = 1 - 2 * odd
    mate = f + sign
    other = (f - sign + frames) % frames
    ahead = (f + 2 * sign + frames) % frames
    behind = (f - 2 * sign + frames) % frames
    d = (c + SWAP) % 2
    u = jnp.where(d == 0, line - 1 - l, l)
    my_d = jnp.where(l < reach, 0, 1)
    my_r = jnp.where(l < reach, l, line - 1 - l)

    def chip(d, steps):
        return jnp.where(d == 0, line - 1 - steps, steps)

    def at(frame, chip, core):
        return {"frame": frame, "pix": 2 * chip + core}

    def entry(r):
        return jnp.where(r >= reach - EARLY, 0, MID)

    barrier = pltpu.get_barrier_semaphore()

    def greet(frame, chip, core):
        pl.semaphore_signal(barrier, inc=1, device_id=at(frame, chip, core), device_id_type=MESH)

    for r in range(reach):
        @pl.when(u == entry(r))
        def _():
            for core in (0, 1):
                source = jnp.where(d == 0, r, line - 1 - r)
                greet(mate, source, core)
                greet(other, source, core)

    greet(f, l, 1 - c)
    greet(ahead, l, c)
    greet(behind, l, c)

    @pl.when(u > 0)
    def _():
        greet(f, chip(d, u - 1), c)

    @pl.when(u < MID)
    def _():
        greet(f, chip(d, u + 1), c)

    onward = jnp.where(u < line - 1, 1, 0)
    backward = jnp.where((u >= 1) & (u <= MID), 1, 0)
    pl.semaphore_wait(barrier, 5 + onward + backward)

    def number(r, core, kind, sub):
        return (((reach - 1 - r) * SUB + sub) * 2 + core) * 2 + kind

    def fields(k):
        return reach - 1 - k // (4 * SUB), k // 2 % 2, k % 2, k // 4 % SUB

    def rows(kind, sub):
        return pl.ds(pl.multiple_of(kind * half + sub * piece, piece), piece)

    def slot_of(kind):
        return jnp.where(kind == 0, odd, 1 - odd)

    def place(slot, k):
        r, core, kind, sub = fields(k)
        source = jnp.where(d == 0, r, line - 1 - r)
        return t.at[slot, 2 * source + core, rows(kind, sub)]

    def first(kind, sub):
        k = number(my_r, c, kind, sub)
        return pltpu.make_async_remote_copy(
            src_ref=own.at[rows(kind, sub)],
            dst_ref=t.at[odd if kind else 1 - odd, p, rows(kind, sub)],
            send_sem=init_send.at[kind, sub],
            recv_sem=chain_recv.at[k],
            device_id=at(other if kind else mate, chip(my_d, entry(my_r)), (my_d + SWAP) % 2),
            device_id_type=MESH,
        )

    def chained(k, step):
        ref = place(slot_of(k % 2), k)
        return pltpu.make_async_remote_copy(
            src_ref=ref,
            dst_ref=ref,
            send_sem=(on_send if step > 0 else back_send).at[k],
            recv_sem=chain_recv.at[k],
            device_id=at(f, chip(d, jnp.clip(u + step, 0, line - 1)), c),
            device_id_type=MESH,
        )

    def sideways(k):
        kind = k % 2
        return pltpu.make_async_remote_copy(
            src_ref=place(slot_of(kind), k),
            dst_ref=place(1 - slot_of(kind), k),
            send_sem=x_send.at[k],
            recv_sem=x_recv.at[k],
            device_id=at(jnp.where(kind == 0, ahead, behind), l, c),
            device_id_type=MESH,
        )

    def across(via, k, mine=True):
        kind = k % 2
        slot = slot_of(kind) if via == 0 else 1 - slot_of(kind)
        r, core, kind, sub = fields(k)
        low = jnp.where((d == 0) == mine, r, line - 1 - r)
        ref = t.at[slot, 2 * low + core, rows(kind, sub)]
        return pltpu.make_async_remote_copy(
            src_ref=ref,
            dst_ref=ref,
            send_sem=p_send.at[via, k],
            recv_sem=p_recv.at[via, k],
            device_id=at(f, l, 1 - c),
            device_id_type=MESH,
        )

    for sub in range(SUB):
        for kind in (0, 1):
            first(kind, sub).start()

    def goes_on(k):
        return (u >= entry(fields(k)[0])) & (u < line - 1)

    def goes_back(k):
        return (u <= entry(fields(k)[0])) & (u > 0)

    def each(count, body):
        if UNROLL:
            for n in range(count):
                body(n)
        else:
            pl.loop(0, count)(body)

    def when(condition, body):
        if isinstance(condition, bool):
            if condition:
                body()
        else:
            pl.when(condition)(body)

    turn = jnp.where(u >= MID, 4 * SUB * EARLY, 0) if MID > 0 else 0

    def step(n):
        def arrived():
            k = (n + turn) % chunks
            chained(k, 1).wait_recv()
            pl.when(goes_on(k))(lambda: chained(k, 1).start())
            if MID > 0:
                pl.when(goes_back(k))(lambda: chained(k, -1).start())
            sideways(k).start()
            across(0, k).start()

        def came_over():
            k = (n - SIDE + turn) % chunks
            sideways(k).wait_recv()
            across(1, k).start()

        when(n < chunks, arrived)
        when(n >= SIDE, came_over)

    each(chunks + SIDE, step)

    def last(k):
        for via in (0, 1):
            across(via, k, False).wait_recv()

    each(chunks, last)

    for sub in range(SUB):
        for kind in (0, 1):
            first(kind, sub).wait_send()

    def sent(k):
        pl.when(goes_on(k))(lambda: chained(k, 1).wait_send())
        if MID > 0:
            pl.when(goes_back(k))(lambda: chained(k, -1).wait_send())
        sideways(k).wait_send()
        for via in (0, 1):
            across(via, k).wait_send()

    each(chunks, sent)


def gather(own, frames, line):
    chunks = 2 * SUB * line
    dma = pltpu.SemaphoreType.DMA
    return pl.pallas_call(
        functools.partial(gather_kernel, frames, line),
        out_shape=pltpu.VMEM((2, 2 * line, *own.shape), own.dtype),
        in_specs=[pl.BlockSpec(memory_space=pltpu.VMEM)],
        out_specs=pl.BlockSpec(memory_space=pltpu.VMEM),
        scratch_shapes=[dma((2, SUB))] + [dma((chunks,))] * 3 + [dma((2, chunks))] + [dma((chunks,))] * 2 + [dma((2, chunks))],
        compiler_params=pltpu.CompilerParams(collective_id=0, has_side_effects=True),
        name="gather",
    )(own)


def pooling(out_rows, out_breadth):
    shape = (out_rows * out_breadth, 4 * out_rows * out_breadth)
    i = lax.broadcasted_iota(jnp.int32, shape, 0)
    q = lax.broadcasted_iota(jnp.int32, shape, 1)
    breadth = 2 * out_breadth
    row, column = q // breadth, q % breadth
    same = (row // 2 == i // out_breadth) & (column // 2 == i % out_breadth)
    return jnp.where(same, 0.25, 0.0).astype(jnp.bfloat16)


NT = (((1,), (1,)), ((), ()))


def dot(a, b):
    return jnp.dot(a, b, preferred_element_type=jnp.float32)


def dot_nt(a, b):
    return lax.dot_general(a, b, NT, preferred_element_type=jnp.float32)


def pyramid_kernel(frames, breadth, own, t, *rest):
    outs, (high1, low1, high2, low2) = rest[:8], rest[8:]
    f = lax.axis_index("frame")
    pixels = own.shape[0]
    rows = pixels // breadth
    targets = t.shape[1]
    factor = 1.0 / math.sqrt(own.shape[1])

    def put(ref, start, values):
        size = values.shape[1]
        for row in range(rows):
            ref[0, row, :, start:start + size] = values[row * breadth:(row + 1) * breadth]

    pool1 = pooling(1, breadth // 2)
    pool2 = pooling(2, breadth // 4)
    pool3 = pooling(4, breadth // 8)
    small = pool1.shape[0]

    def split(values):
        high = values.astype(jnp.bfloat16)
        return high, (values - high.astype(jnp.float32)).astype(jnp.bfloat16)

    for slot in (0, 1):
        valid = jnp.where(f < frames - 1, 1, 0) if slot == 0 else jnp.where(f > 0, 1, 0)
        scale = valid.astype(jnp.float32) * factor
        full, half, quarter, eighth = outs[4 * slot:4 * slot + 4]
        tile = 4 * pixels
        for start in range(0, targets, tile):
            scores = dot_nt(own[...], t[slot, start:start + tile])
            put(full, start, (scores * scale).astype(jnp.bfloat16))
        for u in range(targets // pixels):
            values = dot(pool1, t[slot, u * pixels:(u + 1) * pixels])
            high1[slot, u * small:(u + 1) * small], low1[slot, u * small:(u + 1) * small] = split(values)
        for u in range(targets // 4 // pixels):
            at = slice(u * pixels, (u + 1) * pixels)
            values = dot(pool2, high1[slot, at]) + dot(pool2, low1[slot, at])
            high2[slot, u * small:(u + 1) * small], low2[slot, u * small:(u + 1) * small] = split(values)
        high3, low3 = split(dot(pool3, high2[slot]) + dot(pool3, low2[slot]))
        for ref, high, low in ((half, high1[slot], low1[slot]), (quarter, high2[slot], low2[slot])):
            scores = dot_nt(own[...], high) + dot_nt(own[...], low)
            put(ref, 0, (scores * scale).astype(jnp.bfloat16))
        for row in range(rows):
            mine = own[row * breadth:(row + 1) * breadth]
            scores = dot_nt(high3, mine) + dot_nt(low3, mine)
            eighth[0, row] = (scores * scale).astype(jnp.bfloat16)


def pyramids(own, t, frames, rows, breadth):
    targets = t.shape[1]
    depths = [jax.ShapeDtypeStruct((1, rows, breadth, targets // 4**k), jnp.bfloat16) for k in range(3)]
    depths.append(jax.ShapeDtypeStruct((1, rows, targets // 64, breadth), jnp.bfloat16))
    scratch = [pltpu.VMEM((2, targets // 4**k, own.shape[1]), jnp.bfloat16) for k in (1, 1, 2, 2)]
    return pl.pallas_call(
        functools.partial(pyramid_kernel, frames, breadth),
        out_shape=depths * 2,
        in_specs=[pl.BlockSpec(memory_space=pltpu.VMEM)] * 2,
        out_specs=[pl.BlockSpec(memory_space=pltpu.VMEM)] * 8,
        scratch_shapes=scratch,
        compiler_params=pltpu.CompilerParams(vmem_limit_bytes=32 * 2**20),
        name="pyramids",
    )(own, t)


def solution(mesh):
    frames = mesh.shape["frame"]
    line = mesh.shape["pix"] // 2

    def per_device(features):
        _, rows, breadth, channels = features.shape
        own = features.reshape(rows * breadth, channels)
        t = gather(own, frames, line)
        t = t.reshape(2, -1, channels)
        outs = list(pyramids(own, t, frames, rows, breadth))
        for k in (3, 7):
            outs[k] = outs[k].swapaxes(2, 3)
        return tuple(outs)

    spec = P(("clip", "frame"), "pix", None, None)
    return jax.shard_map(per_device, mesh=mesh, in_specs=(spec,), out_specs=(spec,) * 8, check_vma=False)
```

```python
import functools
import math

import jax
import jax.numpy as jnp
from jax import lax
from jax.experimental import pallas as pl
from jax.experimental.pallas import tpu as pltpu
from jax.sharding import PartitionSpec as P

MESH = pl.DeviceIdType.MESH
SUB = 1
SIDE = 8
SWAP = 1
WAYS = ((3, 1), (2, 2))


def gather_kernel(frames, line, own, t, init_send, on_send, back_send, x_send, p_send, chain_recv, x_recv, p_recv):
    half = own.shape[0] // 2
    piece = half // SUB
    reach = line // 2
    chunks = 4 * SUB * reach
    f = lax.axis_index("frame")
    p = lax.axis_index("pix")
    l = p // 2
    c = p % 2
    odd = f % 2
    sign = 1 - 2 * odd
    mate = f + sign
    other = (f - sign + frames) % frames
    ahead = (f + 2 * sign + frames) % frames
    behind = (f - 2 * sign + frames) % frames
    d = (c + SWAP) % 2
    u = jnp.where(d == 0, line - 1 - l, l)
    my_d = jnp.where(l < reach, 0, 1)
    my_r = jnp.where(l < reach, l, line - 1 - l)

    def chip(d, steps):
        return jnp.where(d == 0, line - 1 - steps, steps)

    def at(frame, chip, core):
        return {"frame": frame, "pix": 2 * chip + core}

    def way_in(parity, chain):
        return jnp.where(
            parity == 0,
            jnp.where(chain == 0, WAYS[0][0], WAYS[0][1]),
            jnp.where(chain == 0, WAYS[1][0], WAYS[1][1]),
        )

    here = way_in(odd, d)
    there = way_in(1 - odd, my_d)
    goes_on = (u >= here) & (u < line - 1)
    goes_back = (u <= here) & (u > 0)

    barrier = pltpu.get_barrier_semaphore()

    def greet(frame, chip, core):
        pl.semaphore_signal(barrier, inc=1, device_id=at(frame, chip, core), device_id_type=MESH)

    @pl.when(u == here)
    def _():
        for r in range(reach):
            for core in (0, 1):
                source = jnp.where(d == 0, r, line - 1 - r)
                greet(mate, source, core)
                greet(other, source, core)

    greet(f, l, 1 - c)
    greet(ahead, l, c)
    greet(behind, l, c)

    @pl.when(u > 0)
    def _():
        greet(f, chip(d, u - 1), c)

    @pl.when(u < line - 1)
    def _():
        greet(f, chip(d, u + 1), c)

    inner = jnp.where((u > 0) & (u < line - 1), 1, 0)
    pl.semaphore_wait(barrier, 6 + inner)

    def number(r, core, kind, sub):
        return (((reach - 1 - r) * SUB + sub) * 2 + core) * 2 + kind

    def fields(k):
        return reach - 1 - k // (4 * SUB), k // 2 % 2, k % 2, k // 4 % SUB

    def rows(kind, sub):
        return pl.ds(pl.multiple_of(kind * half + sub * piece, piece), piece)

    def slot_of(kind):
        return jnp.where(kind == 0, odd, 1 - odd)

    def place(slot, k):
        r, core, kind, sub = fields(k)
        source = jnp.where(d == 0, r, line - 1 - r)
        return t.at[slot, 2 * source + core, rows(kind, sub)]

    def first(kind, sub):
        return pltpu.make_async_remote_copy(
            src_ref=own.at[rows(kind, sub)],
            dst_ref=t.at[odd if kind else 1 - odd, p, rows(kind, sub)],
            send_sem=init_send.at[kind, sub],
            recv_sem=chain_recv.at[number(my_r, c, kind, sub)],
            device_id=at(other if kind else mate, chip(my_d, there), (my_d + SWAP) % 2),
            device_id_type=MESH,
        )

    def chained(k, step):
        ref = place(slot_of(k % 2), k)
        return pltpu.make_async_remote_copy(
            src_ref=ref,
            dst_ref=ref,
            send_sem=(on_send if step > 0 else back_send).at[k],
            recv_sem=chain_recv.at[k],
            device_id=at(f, chip(d, jnp.clip(u + step, 0, line - 1)), c),
            device_id_type=MESH,
        )

    def sideways(k):
        kind = k % 2
        return pltpu.make_async_remote_copy(
            src_ref=place(slot_of(kind), k),
            dst_ref=place(1 - slot_of(kind), k),
            send_sem=x_send.at[k],
            recv_sem=x_recv.at[k],
            device_id=at(jnp.where(kind == 0, ahead, behind), l, c),
            device_id_type=MESH,
        )

    def across(via, k, mine=True):
        kind = k % 2
        slot = slot_of(kind) if via == 0 else 1 - slot_of(kind)
        r, core, kind, sub = fields(k)
        low = jnp.where((d == 0) == mine, r, line - 1 - r)
        ref = t.at[slot, 2 * low + core, rows(kind, sub)]
        return pltpu.make_async_remote_copy(
            src_ref=ref,
            dst_ref=ref,
            send_sem=p_send.at[via, k],
            recv_sem=p_recv.at[via, k],
            device_id=at(f, l, 1 - c),
            device_id_type=MESH,
        )

    firsts = [first(kind, sub) for sub in range(SUB) for kind in (0, 1)]
    for copy in firsts:
        copy.start()

    def arrived(k):
        chained(k, 1).wait_recv()
        pl.when(goes_on)(lambda: chained(k, 1).start())
        pl.when(goes_back)(lambda: chained(k, -1).start())
        sideways(k).start()
        across(0, k).start()

    def came_over(k):
        sideways(k).wait_recv()
        across(1, k).start()

    for n in range(chunks + SIDE):
        if n < chunks:
            arrived(n)
        if n >= SIDE:
            came_over(n - SIDE)

    for k in range(chunks):
        for via in (0, 1):
            across(via, k, False).wait_recv()

    for copy in firsts:
        copy.wait_send()

    for k in range(chunks):
        pl.when(goes_on)(lambda: chained(k, 1).wait_send())
        pl.when(goes_back)(lambda: chained(k, -1).wait_send())
        sideways(k).wait_send()
        for via in (0, 1):
            across(via, k).wait_send()


def gather(own, frames, line):
    chunks = 2 * SUB * line
    dma = pltpu.SemaphoreType.DMA
    return pl.pallas_call(
        functools.partial(gather_kernel, frames, line),
        out_shape=pltpu.VMEM((2, 2 * line, *own.shape), own.dtype),
        in_specs=[pl.BlockSpec(memory_space=pltpu.VMEM)],
        out_specs=pl.BlockSpec(memory_space=pltpu.VMEM),
        scratch_shapes=[dma((2, SUB))] + [dma((chunks,))] * 3 + [dma((2, chunks))] + [dma((chunks,))] * 2 + [dma((2, chunks))],
        compiler_params=pltpu.CompilerParams(collective_id=0, has_side_effects=True),
        name="gather",
    )(own)


def pooling(out_rows, out_breadth):
    shape = (out_rows * out_breadth, 4 * out_rows * out_breadth)
    i = lax.broadcasted_iota(jnp.int32, shape, 0)
    q = lax.broadcasted_iota(jnp.int32, shape, 1)
    breadth = 2 * out_breadth
    row, column = q // breadth, q % breadth
    same = (row // 2 == i // out_breadth) & (column // 2 == i % out_breadth)
    return jnp.where(same, 0.25, 0.0).astype(jnp.bfloat16)


NT = (((1,), (1,)), ((), ()))


def dot(a, b):
    return jnp.dot(a, b, preferred_element_type=jnp.float32)


def dot_nt(a, b):
    return lax.dot_general(a, b, NT, preferred_element_type=jnp.float32)


def pyramid_kernel(frames, breadth, own, t, *rest):
    outs, stage, (high1, low1, high2, low2, sem) = rest[:8], rest[8:16], rest[16:]
    f = lax.axis_index("frame")
    pixels = own.shape[0]
    rows = pixels // breadth
    targets = t.shape[1]
    factor = 1.0 / math.sqrt(own.shape[1])
    copies = []

    def send(index, at):
        copy = pltpu.make_async_copy(stage[index].at[at], outs[index].at[at], sem.at[len(copies)])
        copy.start()
        copies.append(copy)

    def put(index, start, values):
        size = values.shape[1]
        for row in range(rows):
            stage[index][0, row, :, start:start + size] = values[row * breadth:(row + 1) * breadth]
        send(index, (slice(None), slice(None), slice(None), pl.ds(start, size)))

    pool1 = pooling(1, breadth // 2)
    pool2 = pooling(2, breadth // 4)
    pool3 = pooling(4, breadth // 8)
    small = pool1.shape[0]

    def split(values):
        high = values.astype(jnp.bfloat16)
        return high, (values - high.astype(jnp.float32)).astype(jnp.bfloat16)

    scales = []
    for slot in (0, 1):
        valid = jnp.where(f < frames - 1, 1, 0) if slot == 0 else jnp.where(f > 0, 1, 0)
        scales.append(valid.astype(jnp.float32) * factor)
    tile = 4 * pixels
    for slot in (0, 1):
        for start in range(0, targets, tile):
            scores = dot_nt(own[...], t[slot, start:start + tile])
            put(4 * slot, start, (scores * scales[slot]).astype(jnp.bfloat16))
    for slot in (0, 1):
        for v in range(targets // pixels):
            values = dot(pool1, t[slot, v * pixels:(v + 1) * pixels])
            high1[slot, v * small:(v + 1) * small], low1[slot, v * small:(v + 1) * small] = split(values)
        scores = dot_nt(own[...], high1[slot]) + dot_nt(own[...], low1[slot])
        put(4 * slot + 1, 0, (scores * scales[slot]).astype(jnp.bfloat16))
    for slot in (0, 1):
        for v in range(targets // 4 // pixels):
            at = slice(v * pixels, (v + 1) * pixels)
            values = dot(pool2, high1[slot, at]) + dot(pool2, low1[slot, at])
            high2[slot, v * small:(v + 1) * small], low2[slot, v * small:(v + 1) * small] = split(values)
        scores = dot_nt(own[...], high2[slot]) + dot_nt(own[...], low2[slot])
        put(4 * slot + 2, 0, (scores * scales[slot]).astype(jnp.bfloat16))
        high3, low3 = split(dot(pool3, high2[slot]) + dot(pool3, low2[slot]))
        for row in range(rows):
            mine = own[row * breadth:(row + 1) * breadth]
            scores = dot_nt(high3, mine) + dot_nt(low3, mine)
            stage[4 * slot + 3][0, row] = (scores * scales[slot]).astype(jnp.bfloat16)
        send(4 * slot + 3, (slice(None),))
    for copy in copies:
        copy.wait()


def pyramids(own, t, frames, rows, breadth):
    targets = t.shape[1]
    pixels = own.shape[0]
    depths = [(1, rows, breadth, targets // 4**k) for k in range(3)] + [(1, rows, targets // 64, breadth)]
    scratch = [pltpu.VMEM((2, targets // 4**k, own.shape[1]), jnp.bfloat16) for k in (1, 1, 2, 2)]
    return pl.pallas_call(
        functools.partial(pyramid_kernel, frames, breadth),
        out_shape=[jax.ShapeDtypeStruct(shape, jnp.bfloat16) for shape in depths * 2],
        in_specs=[pl.BlockSpec(memory_space=pltpu.VMEM)] * 2,
        out_specs=[pl.BlockSpec(memory_space=pltpu.HBM)] * 8,
        scratch_shapes=[pltpu.VMEM(shape, jnp.bfloat16) for shape in depths * 2]
        + scratch
        + [pltpu.SemaphoreType.DMA((2 * (targets // (4 * pixels) + 3),))],
        compiler_params=pltpu.CompilerParams(vmem_limit_bytes=32 * 2**20),
        name="pyramids",
    )(own, t)


def solution(mesh):
    frames = mesh.shape["frame"]
    line = mesh.shape["pix"] // 2

    def per_device(features):
        _, rows, breadth, channels = features.shape
        own = features.reshape(rows * breadth, channels)
        t = gather(own, frames, line)
        t = t.reshape(2, -1, channels)
        outs = list(pyramids(own, t, frames, rows, breadth))
        for k in (3, 7):
            outs[k] = outs[k].swapaxes(2, 3)
        return tuple(outs)

    spec = P(("clip", "frame"), "pix", None, None)
    return jax.shard_map(per_device, mesh=mesh, in_specs=(spec,), out_specs=(spec,) * 8, check_vma=False)
```

```python
import functools
import math

import jax
import jax.numpy as jnp
from jax import lax
from jax.experimental import pallas as pl
from jax.experimental.pallas import tpu as pltpu
from jax.sharding import PartitionSpec as P

MESH = pl.DeviceIdType.MESH
SUB = 1
SIDE = 8
SWAP = 1
WAYS = ((3, 1), (2, 2))


def pooling(out_rows, out_breadth):
    shape = (out_rows * out_breadth, 4 * out_rows * out_breadth)
    i = lax.broadcasted_iota(jnp.int32, shape, 0)
    q = lax.broadcasted_iota(jnp.int32, shape, 1)
    breadth = 2 * out_breadth
    row, column = q // breadth, q % breadth
    same = (row // 2 == i // out_breadth) & (column // 2 == i % out_breadth)
    return jnp.where(same, 0.25, 0.0).astype(jnp.bfloat16)


NT = (((1,), (1,)), ((), ()))


def dot(a, b):
    return jnp.dot(a, b, preferred_element_type=jnp.float32)


def dot_nt(a, b):
    return lax.dot_general(a, b, NT, preferred_element_type=jnp.float32)


def split(values):
    high = values.astype(jnp.bfloat16)
    return high, (values - high.astype(jnp.float32)).astype(jnp.bfloat16)


def scale_of(frames, slot, channels):
    f = lax.axis_index("frame")
    valid = jnp.where(f < frames - 1, 1, 0) if slot == 0 else jnp.where(f > 0, 1, 0)
    return valid.astype(jnp.float32) * (1.0 / math.sqrt(channels))


def gather_kernel(frames, line, breadth, own, scores0, high1, low1, t, init_send, on_send, back_send, x_send, p_send, chain_recv, x_recv, p_recv):
    half = own.shape[0] // 2
    piece = half // SUB
    reach = line // 2
    chunks = 4 * SUB * reach
    f = lax.axis_index("frame")
    p = lax.axis_index("pix")
    l = p // 2
    c = p % 2
    odd = f % 2
    sign = 1 - 2 * odd
    mate = f + sign
    other = (f - sign + frames) % frames
    ahead = (f + 2 * sign + frames) % frames
    behind = (f - 2 * sign + frames) % frames
    d = (c + SWAP) % 2
    u = jnp.where(d == 0, line - 1 - l, l)
    my_d = jnp.where(l < reach, 0, 1)
    my_r = jnp.where(l < reach, l, line - 1 - l)

    def chip(d, steps):
        return jnp.where(d == 0, line - 1 - steps, steps)

    def at(frame, chip, core):
        return {"frame": frame, "pix": 2 * chip + core}

    def way_in(parity, chain):
        return jnp.where(
            parity == 0,
            jnp.where(chain == 0, WAYS[0][0], WAYS[0][1]),
            jnp.where(chain == 0, WAYS[1][0], WAYS[1][1]),
        )

    here = way_in(odd, d)
    there = way_in(1 - odd, my_d)
    goes_on = (u >= here) & (u < line - 1)
    goes_back = (u <= here) & (u > 0)

    barrier = pltpu.get_barrier_semaphore()

    def greet(frame, chip, core):
        pl.semaphore_signal(barrier, inc=1, device_id=at(frame, chip, core), device_id_type=MESH)

    @pl.when(u == here)
    def _():
        for r in range(reach):
            for core in (0, 1):
                source = jnp.where(d == 0, r, line - 1 - r)
                greet(mate, source, core)
                greet(other, source, core)

    greet(f, l, 1 - c)
    greet(ahead, l, c)
    greet(behind, l, c)

    @pl.when(u > 0)
    def _():
        greet(f, chip(d, u - 1), c)

    @pl.when(u < line - 1)
    def _():
        greet(f, chip(d, u + 1), c)

    inner = jnp.where((u > 0) & (u < line - 1), 1, 0)
    pl.semaphore_wait(barrier, 6 + inner)

    def number(r, core, kind, sub):
        return (((reach - 1 - r) * SUB + sub) * 2 + core) * 2 + kind

    def fields(k):
        return reach - 1 - k // (4 * SUB), k // 2 % 2, k % 2, k // 4 % SUB

    def rows(kind, sub):
        return pl.ds(pl.multiple_of(kind * half + sub * piece, piece), piece)

    def slot_of(kind):
        return jnp.where(kind == 0, odd, 1 - odd)

    def place(slot, k):
        r, core, kind, sub = fields(k)
        source = jnp.where(d == 0, r, line - 1 - r)
        return t.at[slot, 2 * source + core, rows(kind, sub)]

    def first(kind, sub):
        return pltpu.make_async_remote_copy(
            src_ref=own.at[rows(kind, sub)],
            dst_ref=t.at[odd if kind else 1 - odd, p, rows(kind, sub)],
            send_sem=init_send.at[kind, sub],
            recv_sem=chain_recv.at[number(my_r, c, kind, sub)],
            device_id=at(other if kind else mate, chip(my_d, there), (my_d + SWAP) % 2),
            device_id_type=MESH,
        )

    def chained(k, step):
        ref = place(slot_of(k % 2), k)
        return pltpu.make_async_remote_copy(
            src_ref=ref,
            dst_ref=ref,
            send_sem=(on_send if step > 0 else back_send).at[k],
            recv_sem=chain_recv.at[k],
            device_id=at(f, chip(d, jnp.clip(u + step, 0, line - 1)), c),
            device_id_type=MESH,
        )

    def sideways(k):
        kind = k % 2
        return pltpu.make_async_remote_copy(
            src_ref=place(slot_of(kind), k),
            dst_ref=place(1 - slot_of(kind), k),
            send_sem=x_send.at[k],
            recv_sem=x_recv.at[k],
            device_id=at(jnp.where(kind == 0, ahead, behind), l, c),
            device_id_type=MESH,
        )

    def across(via, k, mine=True):
        kind = k % 2
        slot = slot_of(kind) if via == 0 else 1 - slot_of(kind)
        r, core, kind, sub = fields(k)
        low = jnp.where((d == 0) == mine, r, line - 1 - r)
        ref = t.at[slot, 2 * low + core, rows(kind, sub)]
        return pltpu.make_async_remote_copy(
            src_ref=ref,
            dst_ref=ref,
            send_sem=p_send.at[via, k],
            recv_sem=p_recv.at[via, k],
            device_id=at(f, l, 1 - c),
            device_id_type=MESH,
        )

    firsts = [first(kind, sub) for sub in range(SUB) for kind in (0, 1)]
    for copy in firsts:
        copy.start()

    def arrived(k):
        chained(k, 1).wait_recv()
        pl.when(goes_on)(lambda: chained(k, 1).start())
        pl.when(goes_back)(lambda: chained(k, -1).start())
        sideways(k).start()
        across(0, k).start()

    def came_over(k):
        sideways(k).wait_recv()
        across(1, k).start()

    pixels, channels = own.shape
    pool1 = pooling(1, breadth // 2)
    small = pool1.shape[0]

    def use(group, mine):
        r = reach - 1 - group
        source = jnp.where((d == 0) == mine, r, line - 1 - r)
        for slot in (0, 1):
            targets = t[slot, pl.ds(2 * source, 2)].reshape(2 * pixels, channels)
            scores = (dot_nt(own[...], targets) * scale_of(frames, slot, channels)).astype(jnp.bfloat16)
            columns = pl.ds(pl.multiple_of(2 * pixels * source, 128), 2 * pixels)
            for row in range(pixels // breadth):
                scores0[slot, 0, row, :, columns] = scores[row * breadth:(row + 1) * breadth]
            for core in (0, 1):
                values = dot(pool1, targets[core * pixels:(core + 1) * pixels])
                at = pl.ds(pl.multiple_of((2 * source + core) * small, small), small)
                high1[slot, at], low1[slot, at] = split(values)

    per_group = 4 * SUB

    def use_across(group):
        for k in range(per_group * group, per_group * (group + 1)):
            for via in (0, 1):
                across(via, k, False).wait_recv()
        use(group, False)

    for n in range(chunks + SIDE):
        if n < chunks:
            arrived(n)
        if n >= SIDE:
            came_over(n - SIDE)
            if (n - SIDE) % per_group == per_group - 1:
                group = (n - SIDE) // per_group
                pl.when(u >= reach)(lambda: use_across(group))
                use(group, True)

    @pl.when(u < reach)
    def _():
        for group in range(reach):
            use_across(group)

    for copy in firsts:
        copy.wait_send()

    for k in range(chunks):
        pl.when(goes_on)(lambda: chained(k, 1).wait_send())
        pl.when(goes_back)(lambda: chained(k, -1).wait_send())
        sideways(k).wait_send()
        for via in (0, 1):
            across(via, k).wait_send()


def gather(own, frames, line, breadth):
    pixels, channels = own.shape
    targets = 2 * line * pixels
    chunks = 2 * SUB * line
    dma = pltpu.SemaphoreType.DMA
    averages = pltpu.VMEM((2, targets // 4, channels), own.dtype)
    return pl.pallas_call(
        functools.partial(gather_kernel, frames, line, breadth),
        out_shape=[pltpu.VMEM((2, 1, pixels // breadth, breadth, targets), own.dtype), averages, averages],
        in_specs=[pl.BlockSpec(memory_space=pltpu.VMEM)],
        out_specs=[pl.BlockSpec(memory_space=pltpu.VMEM)] * 3,
        scratch_shapes=[pltpu.VMEM((2, 2 * line, *own.shape), own.dtype)]
        + [dma((2, SUB))] + [dma((chunks,))] * 3 + [dma((2, chunks))] + [dma((chunks,))] * 2 + [dma((2, chunks))],
        compiler_params=pltpu.CompilerParams(collective_id=0, has_side_effects=True, vmem_limit_bytes=32 * 2**20),
        name="gather",
    )(own)


def pyramid_kernel(frames, breadth, own, scores0, high1, low1, *rest):
    outs, stage, (high2, low2, sem) = rest[:8], rest[8:14], rest[14:]
    pixels, channels = own.shape
    rows = pixels // breadth
    copies = []

    def send(source, target):
        copy = pltpu.make_async_copy(source, target, sem.at[len(copies)])
        copy.start()
        copies.append(copy)

    for slot in (0, 1):
        send(scores0.at[slot], outs[4 * slot])

    pool2 = pooling(2, breadth // 4)
    pool3 = pooling(4, breadth // 8)
    small = pool2.shape[0]

    for slot in (0, 1):
        half, quarter, eighth = stage[3 * slot:3 * slot + 3]
        scale = scale_of(frames, slot, channels)

        def put(ref, out, high, low):
            scores = dot_nt(own[...], high) + dot_nt(own[...], low)
            scores = (scores * scale).astype(jnp.bfloat16)
            for row in range(rows):
                ref[0, row] = scores[row * breadth:(row + 1) * breadth]
            send(ref, out)

        put(half, outs[4 * slot + 1], high1[slot], low1[slot])
        for v in range(high1.shape[1] // pixels):
            at = slice(v * pixels, (v + 1) * pixels)
            values = dot(pool2, high1[slot, at]) + dot(pool2, low1[slot, at])
            high2[slot, v * small:(v + 1) * small], low2[slot, v * small:(v + 1) * small] = split(values)
        put(quarter, outs[4 * slot + 2], high2[slot], low2[slot])
        high3, low3 = split(dot(pool3, high2[slot]) + dot(pool3, low2[slot]))
        for row in range(rows):
            mine = own[row * breadth:(row + 1) * breadth]
            scores = dot_nt(high3, mine) + dot_nt(low3, mine)
            eighth[0, row] = (scores * scale).astype(jnp.bfloat16)
        send(eighth, outs[4 * slot + 3])
    for copy in copies:
        copy.wait()


def pyramids(own, scores0, high1, low1, frames):
    _, _, rows, breadth, targets = scores0.shape
    depths = [(1, rows, breadth, targets // 4**k) for k in range(3)] + [(1, rows, targets // 64, breadth)]
    return pl.pallas_call(
        functools.partial(pyramid_kernel, frames, breadth),
        out_shape=[jax.ShapeDtypeStruct(shape, jnp.bfloat16) for shape in depths * 2],
        in_specs=[pl.BlockSpec(memory_space=pltpu.VMEM)] * 4,
        out_specs=[pl.BlockSpec(memory_space=pltpu.HBM)] * 8,
        scratch_shapes=[pltpu.VMEM(shape, jnp.bfloat16) for shape in depths[1:] * 2]
        + [pltpu.VMEM((2, targets // 16, own.shape[1]), jnp.bfloat16)] * 2
        + [pltpu.SemaphoreType.DMA((8,))],
        compiler_params=pltpu.CompilerParams(vmem_limit_bytes=32 * 2**20),
        name="pyramids",
    )(own, scores0, high1, low1)


def solution(mesh):
    frames = mesh.shape["frame"]
    line = mesh.shape["pix"] // 2

    def per_device(features):
        _, rows, breadth, channels = features.shape
        own = features.reshape(rows * breadth, channels)
        outs = list(pyramids(own, *gather(own, frames, line, breadth), frames))
        for k in (3, 7):
            outs[k] = outs[k].swapaxes(2, 3)
        return tuple(outs)

    spec = P(("clip", "frame"), "pix", None, None)
    return jax.shard_map(per_device, mesh=mesh, in_specs=(spec,), out_specs=(spec,) * 8, check_vma=False)
```

```python
import functools
import math

import jax
import jax.numpy as jnp
from jax import lax
from jax.experimental import pallas as pl
from jax.experimental.pallas import tpu as pltpu
from jax.sharding import PartitionSpec as P

MESH = pl.DeviceIdType.MESH
SUB = 1
SIDE = 8
WAYS = ((3, 1), (2, 2))


def pooling(out_rows, out_breadth):
    shape = (out_rows * out_breadth, 4 * out_rows * out_breadth)
    i = lax.broadcasted_iota(jnp.int32, shape, 0)
    q = lax.broadcasted_iota(jnp.int32, shape, 1)
    breadth = 2 * out_breadth
    row, column = q // breadth, q % breadth
    same = (row // 2 == i // out_breadth) & (column // 2 == i % out_breadth)
    return jnp.where(same, 0.25, 0.0).astype(jnp.bfloat16)


NT = (((1,), (1,)), ((), ()))


def dot(a, b):
    return jnp.dot(a, b, preferred_element_type=jnp.float32)


def dot_nt(a, b):
    return lax.dot_general(a, b, NT, preferred_element_type=jnp.float32)


def split(values):
    high = values.astype(jnp.bfloat16)
    return high, (values - high.astype(jnp.float32)).astype(jnp.bfloat16)


def scale_of(frames, slot, channels):
    f = lax.axis_index("frame")
    valid = jnp.where(f < frames - 1, 1, 0) if slot == 0 else jnp.where(f > 0, 1, 0)
    return valid.astype(jnp.float32) * (1.0 / math.sqrt(channels))


def gather_kernel(frames, line, breadth, own, scores0, high1, low1, t, init_send, on_send, back_send, x_send, p_send, chain_recv, x_recv, p_recv):
    half = own.shape[0] // 2
    piece = half // SUB
    reach = line // 2
    chunks = 4 * SUB * reach
    f = lax.axis_index("frame")
    p = lax.axis_index("pix")
    l = p // 2
    c = p % 2
    odd = f % 2
    sign = 1 - 2 * odd
    mate = f + sign
    other = (f - sign + frames) % frames
    ahead = (f + 2 * sign + frames) % frames
    behind = (f - 2 * sign + frames) % frames
    d = (c + 1 - odd) % 2
    u = jnp.where(d == 0, line - 1 - l, l)
    my_d = jnp.where(l < reach, 0, 1)
    my_r = jnp.where(l < reach, l, line - 1 - l)

    def chip(d, steps):
        return jnp.where(d == 0, line - 1 - steps, steps)

    def at(frame, chip, core):
        return {"frame": frame, "pix": 2 * chip + core}

    def way_in(parity, chain):
        return jnp.where(
            parity == 0,
            jnp.where(chain == 0, WAYS[0][0], WAYS[0][1]),
            jnp.where(chain == 0, WAYS[1][0], WAYS[1][1]),
        )

    here = way_in(odd, d)
    there = way_in(1 - odd, my_d)
    goes_on = (u >= here) & (u < line - 1)
    goes_back = (u <= here) & (u > 0)

    barrier = pltpu.get_barrier_semaphore()

    def greet(frame, chip, core):
        pl.semaphore_signal(barrier, inc=1, device_id=at(frame, chip, core), device_id_type=MESH)

    @pl.when(u == here)
    def _():
        for r in range(reach):
            for core in (0, 1):
                source = jnp.where(d == 0, r, line - 1 - r)
                greet(mate, source, core)
                greet(other, source, core)

    greet(f, l, 1 - c)
    greet(ahead, l, c)
    greet(behind, l, c)

    @pl.when(u > 0)
    def _():
        greet(f, chip(d, u - 1), c)

    @pl.when(u < line - 1)
    def _():
        greet(f, chip(d, u + 1), c)

    inner = jnp.where((u > 0) & (u < line - 1), 1, 0)
    pl.semaphore_wait(barrier, 6 + inner)

    def number(r, core, kind, sub):
        return (((reach - 1 - r) * SUB + sub) * 2 + core) * 2 + kind

    def fields(k):
        return reach - 1 - k // (4 * SUB), k // 2 % 2, k % 2, k // 4 % SUB

    def rows(kind, sub):
        return pl.ds(pl.multiple_of(kind * half + sub * piece, piece), piece)

    def slot_of(kind):
        return jnp.where(kind == 0, odd, 1 - odd)

    def place(slot, k):
        r, core, kind, sub = fields(k)
        source = jnp.where(d == 0, r, line - 1 - r)
        return t.at[slot, 2 * source + core, rows(kind, sub)]

    def first(kind, sub):
        return pltpu.make_async_remote_copy(
            src_ref=own.at[rows(kind, sub)],
            dst_ref=t.at[odd if kind else 1 - odd, p, rows(kind, sub)],
            send_sem=init_send.at[kind, sub],
            recv_sem=chain_recv.at[number(my_r, c, kind, sub)],
            device_id=at(other if kind else mate, chip(my_d, there), (my_d + odd) % 2),
            device_id_type=MESH,
        )

    def chained(k, step):
        ref = place(slot_of(k % 2), k)
        return pltpu.make_async_remote_copy(
            src_ref=ref,
            dst_ref=ref,
            send_sem=(on_send if step > 0 else back_send).at[k],
            recv_sem=chain_recv.at[k],
            device_id=at(f, chip(d, jnp.clip(u + step, 0, line - 1)), c),
            device_id_type=MESH,
        )

    def sideways(k):
        kind = k % 2
        return pltpu.make_async_remote_copy(
            src_ref=place(slot_of(kind), k),
            dst_ref=place(1 - slot_of(kind), k),
            send_sem=x_send.at[k],
            recv_sem=x_recv.at[k],
            device_id=at(jnp.where(kind == 0, ahead, behind), l, c),
            device_id_type=MESH,
        )

    def across(via, k, mine=True):
        kind = k % 2
        slot = slot_of(kind) if via == 0 else 1 - slot_of(kind)
        r, core, kind, sub = fields(k)
        low = jnp.where((d == 0) == mine, r, line - 1 - r)
        ref = t.at[slot, 2 * low + core, rows(kind, sub)]
        return pltpu.make_async_remote_copy(
            src_ref=ref,
            dst_ref=ref,
            send_sem=p_send.at[via, k],
            recv_sem=p_recv.at[via, k],
            device_id=at(f, l, 1 - c),
            device_id_type=MESH,
        )

    firsts = [first(kind, sub) for sub in range(SUB) for kind in (0, 1)]
    for copy in firsts:
        copy.start()

    def arrived(k):
        chained(k, 1).wait_recv()
        pl.when(goes_on)(lambda: chained(k, 1).start())
        pl.when(goes_back)(lambda: chained(k, -1).start())
        sideways(k).start()
        across(0, k).start()

    def came_over(k):
        sideways(k).wait_recv()
        across(1, k).start()

    pixels, channels = own.shape
    pool1 = pooling(1, breadth // 2)
    small = pool1.shape[0]

    def use(group, mine):
        r = reach - 1 - group
        source = jnp.where((d == 0) == mine, r, line - 1 - r)
        for slot in (0, 1):
            targets = t[slot, pl.ds(2 * source, 2)].reshape(2 * pixels, channels)
            scores = (dot_nt(own[...], targets) * scale_of(frames, slot, channels)).astype(jnp.bfloat16)
            columns = pl.ds(pl.multiple_of(2 * pixels * source, 128), 2 * pixels)
            for row in range(pixels // breadth):
                scores0[slot, 0, row, :, columns] = scores[row * breadth:(row + 1) * breadth]
            for core in (0, 1):
                values = dot(pool1, targets[core * pixels:(core + 1) * pixels])
                at = pl.ds(pl.multiple_of((2 * source + core) * small, small), small)
                high1[slot, at], low1[slot, at] = split(values)

    per_group = 4 * SUB

    def use_across(group):
        for k in range(per_group * group, per_group * (group + 1)):
            for via in (0, 1):
                across(via, k, False).wait_recv()
        use(group, False)

    for n in range(chunks + SIDE):
        if n < chunks:
            arrived(n)
        if n >= SIDE:
            came_over(n - SIDE)
            if (n - SIDE) % per_group == per_group - 1:
                group = (n - SIDE) // per_group
                pl.when(u >= reach)(lambda: use_across(group))
                use(group, True)

    @pl.when(u < reach)
    def _():
        for group in range(reach):
            use_across(group)

    for copy in firsts:
        copy.wait_send()

    for k in range(chunks):
        pl.when(goes_on)(lambda: chained(k, 1).wait_send())
        pl.when(goes_back)(lambda: chained(k, -1).wait_send())
        sideways(k).wait_send()
        for via in (0, 1):
            across(via, k).wait_send()


def gather(own, frames, line, breadth):
    pixels, channels = own.shape
    targets = 2 * line * pixels
    chunks = 2 * SUB * line
    dma = pltpu.SemaphoreType.DMA
    averages = pltpu.VMEM((2, targets // 4, channels), own.dtype)
    return pl.pallas_call(
        functools.partial(gather_kernel, frames, line, breadth),
        out_shape=[pltpu.VMEM((2, 1, pixels // breadth, breadth, targets), own.dtype), averages, averages],
        in_specs=[pl.BlockSpec(memory_space=pltpu.VMEM)],
        out_specs=[pl.BlockSpec(memory_space=pltpu.VMEM)] * 3,
        scratch_shapes=[pltpu.VMEM((2, 2 * line, *own.shape), own.dtype)]
        + [dma((2, SUB))] + [dma((chunks,))] * 3 + [dma((2, chunks))] + [dma((chunks,))] * 2 + [dma((2, chunks))],
        compiler_params=pltpu.CompilerParams(collective_id=0, has_side_effects=True, vmem_limit_bytes=32 * 2**20),
        name="gather",
    )(own)


def pyramid_kernel(frames, breadth, own, scores0, high1, low1, *rest):
    outs, stage, (high2, low2, sem) = rest[:8], rest[8:14], rest[14:]
    pixels, channels = own.shape
    rows = pixels // breadth
    copies = []

    def send(source, target):
        copy = pltpu.make_async_copy(source, target, sem.at[len(copies)])
        copy.start()
        copies.append(copy)

    for slot in (0, 1):
        send(scores0.at[slot], outs[4 * slot])

    pool2 = pooling(2, breadth // 4)
    pool3 = pooling(4, breadth // 8)
    small = pool2.shape[0]

    for slot in (0, 1):
        half, quarter, eighth = stage[3 * slot:3 * slot + 3]
        scale = scale_of(frames, slot, channels)

        def put(ref, out, high, low):
            scores = dot_nt(own[...], high) + dot_nt(own[...], low)
            scores = (scores * scale).astype(jnp.bfloat16)
            for row in range(rows):
                ref[0, row] = scores[row * breadth:(row + 1) * breadth]
            send(ref, out)

        put(half, outs[4 * slot + 1], high1[slot], low1[slot])
        for v in range(high1.shape[1] // pixels):
            at = slice(v * pixels, (v + 1) * pixels)
            values = dot(pool2, high1[slot, at]) + dot(pool2, low1[slot, at])
            high2[slot, v * small:(v + 1) * small], low2[slot, v * small:(v + 1) * small] = split(values)
        put(quarter, outs[4 * slot + 2], high2[slot], low2[slot])
        high3, low3 = split(dot(pool3, high2[slot]) + dot(pool3, low2[slot]))
        for row in range(rows):
            mine = own[row * breadth:(row + 1) * breadth]
            scores = dot_nt(high3, mine) + dot_nt(low3, mine)
            eighth[0, row] = (scores * scale).astype(jnp.bfloat16)
        send(eighth, outs[4 * slot + 3])
    for copy in copies:
        copy.wait()


def pyramids(own, scores0, high1, low1, frames):
    _, _, rows, breadth, targets = scores0.shape
    depths = [(1, rows, breadth, targets // 4**k) for k in range(3)] + [(1, rows, targets // 64, breadth)]
    return pl.pallas_call(
        functools.partial(pyramid_kernel, frames, breadth),
        out_shape=[jax.ShapeDtypeStruct(shape, jnp.bfloat16) for shape in depths * 2],
        in_specs=[pl.BlockSpec(memory_space=pltpu.VMEM)] * 4,
        out_specs=[pl.BlockSpec(memory_space=pltpu.HBM)] * 8,
        scratch_shapes=[pltpu.VMEM(shape, jnp.bfloat16) for shape in depths[1:] * 2]
        + [pltpu.VMEM((2, targets // 16, own.shape[1]), jnp.bfloat16)] * 2
        + [pltpu.SemaphoreType.DMA((8,))],
        compiler_params=pltpu.CompilerParams(vmem_limit_bytes=32 * 2**20),
        name="pyramids",
    )(own, scores0, high1, low1)


def solution(mesh):
    frames = mesh.shape["frame"]
    line = mesh.shape["pix"] // 2

    def per_device(features):
        _, rows, breadth, channels = features.shape
        own = features.reshape(rows * breadth, channels)
        outs = list(pyramids(own, *gather(own, frames, line, breadth), frames))
        for k in (3, 7):
            outs[k] = outs[k].swapaxes(2, 3)
        return tuple(outs)

    spec = P(("clip", "frame"), "pix", None, None)
    return jax.shard_map(per_device, mesh=mesh, in_specs=(spec,), out_specs=(spec,) * 8, check_vma=False)
```
